512 devices in a mesh: expert: 128 (over z, y_hi, x), half: 4 (over y_lo, core).
Axes of the slice: x: 4, y: 4 (y_hi: 2, y_lo: 2; y = y_hi * 2 + y_lo), z: 16, core: 2. Of those that a mesh axis runs over, the one named last changes fastest.
Arguments:
- tokens: bfloat16 [131072, 1024], P(('expert', 'half')), may hold values from -6 to 6
- router: bfloat16 [1024, 256], replicated, may hold values from -1 to 1
- w_in: bfloat16 [128, 1024, 3072], P('expert', None, 'half'), may hold values from -0.1875 to 0.1875
- w_out: bfloat16 [128, 3072, 1024], P('expert', 'half'), may hold values from -0.109375 to 0.109375
Outputs:
- mixed: bfloat16 [131072, 1024], P(('expert', 'half'))
The draws below stay inside these ranges and needn't reach their ends.
All inputs are finite; a program needn't handle non-finite values.
Results may differ from the reference program's by a relative error of at most 0.018.
Values may be sent and summed in bfloat16 or wider, within the bound.
No kernel may reach another device: no remote copies, remote signals or barrier semaphores. Data moves between devices by JAX's collectives and lax.ppermute only.
A program may use at most 64 MiB of HBM per device.

```python
import jax
import jax.numpy as jnp
from jax import lax

D = 1024
FF = 3072
SLOTS = 2
PATCHES = 256
EXPERTS = 128
IMAGES = 512
TOKENS = 131072
N_HALF = 4


def joint_draw(key):
    base = jax.random.fold_in(key, 7)
    key_tokens, key_router = jax.random.split(base, 2)
    columns = EXPERTS * SLOTS
    tokens = jnp.clip(jax.random.normal(key_tokens, (TOKENS, D), jnp.float32), -6.0, 6.0)
    router = jnp.clip(jax.random.normal(key_router, (D, columns), jnp.float32), -6.0, 6.0) * D ** (-0.5)
    return (tokens, router)


def draw_tokens(key, part):
    return joint_draw(key)[0].astype(jnp.bfloat16)


def draw_router(key, part):
    return joint_draw(key)[1].astype(jnp.bfloat16)


def levels(stream_key, dims, shards, least, high):
    gain, own = 1.0, jax.random.fold_in(stream_key, 6)
    for dim, shards_of in shards:
        heights = jnp.exp(jax.random.uniform(jax.random.fold_in(own, dim), (shards_of,), jnp.float32, least / len(shards), high / len(shards)))
        gain = gain * jnp.repeat(heights, dims[dim] // shards_of).reshape([-1 if axis == dim else 1 for axis in range(len(dims))])
    return gain


def noise(stream_key, dims, spread, reach, shards=(), kind=jnp.bfloat16):
    entries = jax.random.normal(stream_key, dims, jnp.float32) * spread
    if len(shards) > 0:
        entries = levels(stream_key, dims, shards, -0.22, 0.18) * entries
    return jnp.clip(entries, min=-reach, max=reach).astype(kind)


def setup_inputs(seed: int = 0) -> dict:
    seeds = jax.random.split(jax.random.key(seed), 5)
    return {
        "tokens": draw_tokens(jax.random.fold_in(seeds[4], 71), 0),
        "router": draw_router(jax.random.fold_in(seeds[4], 71), 0),
        "w_in": noise(seeds[2], (EXPERTS, D, FF), D ** -0.5, 0.1875, ((0, 128), (2, 4))),
        "w_out": noise(seeds[3], (EXPERTS, FF, D), FF ** -0.5, 0.109375, ((0, 128), (1, 4))),
    }


def expert_apply(operands):
    rows, first, second = operands
    share = FF // N_HALF
    total = jnp.zeros((rows.shape[0], D), jnp.float32)
    for quarter in range(N_HALF):
        left = first[:, quarter * share:(quarter + 1) * share].astype(jnp.float32)
        right = second[quarter * share:(quarter + 1) * share, :].astype(jnp.float32)
        hidden = jax.nn.gelu(jnp.dot(rows.astype(jnp.float32), left, precision=lax.Precision.HIGHEST)).astype(jnp.bfloat16)
        partial_out = jnp.dot(hidden.astype(jnp.float32), right, precision=lax.Precision.HIGHEST).astype(jnp.bfloat16)
        total = total + lax.optimization_barrier(partial_out).astype(jnp.float32)
    return total.astype(jnp.bfloat16)


def reference(tokens, router, w_in, w_out):
    columns = EXPERTS * SLOTS
    picture = tokens.reshape(IMAGES, PATCHES, D).astype(jnp.float32)
    logits = jnp.einsum("imd,dc->imc", picture, router.astype(jnp.float32), precision=lax.Precision.HIGHEST)
    dispatch = jax.nn.softmax(logits, axis=1).astype(jnp.bfloat16)
    combine = jax.nn.softmax(logits, axis=2).astype(jnp.bfloat16)
    slot_input = jnp.einsum("imc,imd->icd", dispatch.astype(jnp.float32), picture, precision=lax.Precision.HIGHEST).astype(jnp.bfloat16)
    per_expert = slot_input.reshape(IMAGES, EXPERTS, SLOTS, D).transpose(1, 0, 2, 3).reshape(EXPERTS, IMAGES * SLOTS, D)
    outputs = lax.map(expert_apply, (per_expert, w_in, w_out))
    slot_output = outputs.reshape(EXPERTS, IMAGES, SLOTS, D).transpose(1, 0, 2, 3).reshape(IMAGES, columns, D)
    mixed = jnp.einsum("imc,icd->imd", combine.astype(jnp.float32), slot_output.astype(jnp.float32), precision=lax.Precision.HIGHEST)
    return mixed.astype(jnp.bfloat16).reshape(TOKENS, D)
```

```python
import jax
import jax.numpy as jnp
from jax import lax
from jax.sharding import PartitionSpec as P

SLOTS = 2
PIECES = 2


OTHER_CORE = [(0, 1), (1, 0), (2, 3), (3, 2)]
OTHER_CHIP = [(0, 2), (1, 3), (2, 0), (3, 1)]


def experts_half(rows, first, second):
    hidden = jax.nn.gelu(
        jnp.einsum("rd,df->rf", rows, first, preferred_element_type=jnp.float32)
    ).astype(jnp.bfloat16)
    return jnp.einsum("rf,fd->rd", hidden, second, preferred_element_type=jnp.float32)


def on_device(tokens, router, w_in, w_out):
    width = tokens.shape[1]
    experts_all = router.shape[1] // SLOTS
    logits = jnp.einsum("md,dc->mc", tokens, router, preferred_element_type=jnp.float32)
    dispatch = jax.nn.softmax(logits, axis=0).astype(jnp.bfloat16)
    combine = jax.nn.softmax(logits, axis=1).astype(jnp.bfloat16)
    slot_input = jnp.einsum(
        "mc,md->cd", dispatch, tokens, preferred_element_type=jnp.float32
    ).astype(jnp.bfloat16)
    arrived = lax.all_to_all(
        slot_input.reshape(experts_all, SLOTS, width), "expert", 0, 0, tiled=True
    )
    rows = arrived.reshape(-1, width)
    first = jnp.concatenate([w_in[0], lax.ppermute(w_in[0], "half", OTHER_CORE)], axis=1)
    second = jnp.concatenate([w_out[0], lax.ppermute(w_out[0], "half", OTHER_CORE)], axis=0)
    pieces = jnp.split(rows, PIECES)
    others = [lax.ppermute(piece, "half", OTHER_CHIP) for piece in pieces]
    own = experts_half(rows, first, second)
    own, others[0] = lax.optimization_barrier((own, others[0]))
    terms = [experts_half(piece, first, second).astype(jnp.bfloat16) for piece in others]
    returned = [lax.ppermute(term, "half", OTHER_CHIP) for term in terms]
    result = (own + jnp.concatenate(returned).astype(jnp.float32)).astype(jnp.bfloat16)
    slot_output = lax.all_to_all(
        result.reshape(experts_all, SLOTS, width), "expert", 0, 0, tiled=True
    ).reshape(-1, width)
    return jnp.einsum(
        "mc,cd->md", combine, slot_output, preferred_element_type=jnp.float32
    ).astype(jnp.bfloat16)


def solution(mesh):
    return jax.shard_map(
        on_device,
        mesh=mesh,
        in_specs=(
            P(("expert", "half"), None),
            P(),
            P("expert", None, "half"),
            P("expert", "half", None),
        ),
        out_specs=P(("expert", "half"), None),
        check_vma=False,
    )
```

```python
import jax
import jax.numpy as jnp
from jax import lax
from jax.experimental import pallas as pl
from jax.experimental.pallas import tpu as pltpu
from jax.sharding import PartitionSpec as P


SLOTS = 2
PIECES = 2


OTHER_CORE = [(0, 1), (1, 0), (2, 3), (3, 2)]
OTHER_CHIP = [(0, 2), (1, 3), (2, 0), (3, 1)]


def mlp_kernel(rows_ref, in_ref, out_ref, terms_ref):
    rows = rows_ref[...]
    hidden = jax.nn.gelu(jnp.dot(rows, in_ref[...], preferred_element_type=jnp.float32))
    terms_ref[...] = jnp.dot(
        hidden.astype(jnp.bfloat16), out_ref[...], preferred_element_type=jnp.float32
    ).astype(terms_ref.dtype)


def loader_kernel(in_a, in_b, out_a, out_b, in_ref, out_ref, sems):
    units = in_a.shape[1]
    copies = [
        pltpu.make_async_copy(source, target, sems.at[k])
        for k, (source, target) in enumerate(
            (
                (in_a, in_ref.at[:, pl.ds(0, units)]),
                (in_b, in_ref.at[:, pl.ds(units, units)]),
                (out_a, out_ref.at[pl.ds(0, units)]),
                (out_b, out_ref.at[pl.ds(units, units)]),
            )
        )
    ]
    for copy in copies:
        copy.start()
    for copy in copies:
        copy.wait()


def side_by_side(in_a, in_b, out_a, out_b):
    width, units = in_a.shape
    size = 4 * width * 2 * units
    return pl.pallas_call(
        loader_kernel,
        out_shape=[
            pltpu.VMEM((width, 2 * units), jnp.bfloat16),
            pltpu.VMEM((2 * units, width), jnp.bfloat16),
        ],
        in_specs=[pl.BlockSpec(memory_space=pltpu.HBM)] * 4,
        out_specs=[pl.BlockSpec(memory_space=pltpu.VMEM)] * 2,
        scratch_shapes=[pltpu.SemaphoreType.DMA((4,))],
        compiler_params=pltpu.CompilerParams(vmem_limit_bytes=16 << 20),
        cost_estimate=pl.CostEstimate(flops=0, bytes_accessed=2 * size, transcendentals=0),
    )(in_a, in_b, out_a, out_b)


def experts_half(rows, weights, kind):
    count, width = rows.shape
    units = weights[0].shape[1]
    return pl.pallas_call(
        mlp_kernel,
        out_shape=jax.ShapeDtypeStruct((count, width), kind),
        in_specs=[pl.BlockSpec(memory_space=pltpu.VMEM)] * 3,
        out_specs=pl.BlockSpec(memory_space=pltpu.VMEM),
        compiler_params=pltpu.CompilerParams(vmem_limit_bytes=24 << 20),
        cost_estimate=pl.CostEstimate(
            flops=4 * count * width * units,
            bytes_accessed=4 * width * units,
            transcendentals=count * units,
        ),
    )(rows, *weights)


def on_device(tokens, router, w_in, w_out):
    width = tokens.shape[1]
    experts_all = router.shape[1] // SLOTS
    logits = jnp.einsum("md,dc->mc", tokens, router, preferred_element_type=jnp.float32)
    dispatch = jax.nn.softmax(logits, axis=0).astype(jnp.bfloat16)
    combine = jax.nn.softmax(logits, axis=1).astype(jnp.bfloat16)
    slot_input = jnp.einsum(
        "mc,md->cd", dispatch, tokens, preferred_element_type=jnp.float32
    ).astype(jnp.bfloat16)
    arrived = lax.all_to_all(
        slot_input.reshape(experts_all, SLOTS, width), "expert", 0, 0, tiled=True
    )
    rows = lax.optimization_barrier(arrived.reshape(-1, width))
    in_b = lax.ppermute(w_in[0], "half", OTHER_CORE)
    out_b = lax.ppermute(w_out[0], "half", OTHER_CORE)
    weights = side_by_side(w_in[0], in_b, w_out[0], out_b)
    others = []
    for piece in jnp.split(rows, PIECES):
        others.append(lax.ppermute(piece, "half", OTHER_CHIP))
    terms = [experts_half(piece, weights, jnp.bfloat16) for piece in others]
    rows, terms[0] = lax.optimization_barrier((rows, terms[0]))
    own = experts_half(rows, weights, jnp.float32)
    returned = [lax.ppermute(term, "half", OTHER_CHIP) for term in terms]
    result = (own + jnp.concatenate(returned).astype(jnp.float32)).astype(jnp.bfloat16)
    slot_output = lax.all_to_all(
        result.reshape(experts_all, SLOTS, width), "expert", 0, 0, tiled=True
    ).reshape(-1, width)
    return jnp.einsum(
        "mc,cd->md", combine, slot_output, preferred_element_type=jnp.float32
    ).astype(jnp.bfloat16)


def solution(mesh):
    return jax.shard_map(
        on_device,
        mesh=mesh,
        in_specs=(
            P(("expert", "half"), None),
            P(),
            P("expert", None, "half"),
            P("expert", "half", None),
        ),
        out_specs=P(("expert", "half"), None),
        check_vma=False,
    )
```
